32 devices in a mesh: group: 2 (over x), fsdp: 16 (over z, y, core).
Axes of the slice: x: 2, y: 2, z: 4, core: 2. Of those that a mesh axis runs over, the one named last changes fastest.
Arguments:
- tokens: bfloat16 [4096, 4096], P(('group', 'fsdp')), parts along dimension 0, may hold values from -6 to 6
- gate_cot: bfloat16 [4096, 16384], P(('group', 'fsdp')), parts along dimension 0, may hold values from -6 to 6
- gate_weight: bfloat16 [4096, 16384], P(None, 'fsdp'), may hold values from -0.15625 to 0.15625
- keep_mask: int32 [32, 128], P(None, 'fsdp'), may hold values from 0 to 1, as said below
Outputs:
- gate_out: bfloat16 [4096, 16384], P(('group', 'fsdp')), parts along dimension 0
- grad_tiles: bfloat16 [256, 12, 128, 128], P(('group', 'fsdp')), parts along dimension 0
The draws below stay inside these ranges and needn't reach their ends.
There are 2 independent parts, one for each index of `group`. The reference program is written for one: setup_inputs(seed, part) draws one part's arguments, and reference() takes and returns one part's arrays. A program takes and returns all parts, laid end to end along the dimension named above; an argument that names none is the same for every part. Nothing has to cross between parts.
Inputs may be any that keep to these rules, and one draw needn't show every extreme that they name: `keep_mask`: each tile column keeps between 8 and 12 tiles; some column keeps exactly 12.
All inputs are finite; a program needn't handle non-finite values.
Results may differ from the reference program's by a relative error of at most 0.001.
Values may be sent and summed in bfloat16 or wider, within the bound.
A program may use at most 256 MiB of HBM per device.

```python
import jax
import jax.numpy as jnp

D = 4096
FW = 16384
TILE = 128
RT = 32
CT = 128
KMAX = 12
TOKENS = 2048


def draw_keep_mask(key, part):
    base = jax.random.fold_in(key, 11)
    key_count, key_pick, key_order = jax.random.split(base, 3)
    kept_count = jax.random.randint(key_count, (CT,), RT // 4, KMAX + 1)
    chosen = jax.random.randint(key_pick, (), 0, CT)
    kept_count = jnp.where(jnp.arange(CT) == chosen, KMAX, kept_count)
    scores = jax.random.randint(key_order, (RT, CT), 0, 1 << 20) * RT + jnp.arange(RT)[:, None]
    ranking = jnp.argsort(jnp.argsort(scores, axis=0), axis=0)
    return (ranking < kept_count[None, :]).astype(jnp.int32)


def shard_levels(own_key, extent, shards, least, largest):
    loudness = 1.0
    for axis_at, parts in shards:
        steps = jax.random.uniform(jax.random.fold_in(jax.random.fold_in(own_key, 6), axis_at), (parts,), jnp.float32, least / len(shards), largest / len(shards))
        loudness = loudness * jnp.repeat(jnp.exp(steps), extent[axis_at] // parts).reshape((-1,) + (1,) * (len(extent) - 1 - axis_at))
    return loudness


def normal_values(key, shape, spread, bound, pieces=(), held_as=jnp.bfloat16):
    array = jax.random.normal(key, shape, jnp.float32) * spread
    if len(pieces) > 0:
        array = shard_levels(key, shape, pieces, -0.22, 0.18) * array
    return jnp.clip(array, min=-bound, max=bound).astype(held_as)


def setup_inputs(seed: int = 0, part: int = 0) -> dict:
    arg_keys = jax.random.split(jax.random.key(seed), 5)
    part_splits = jax.random.split(jax.random.fold_in(arg_keys[4], part), 5)
    tokens = normal_values(part_splits[0], (TOKENS, D), 1.0, 6.0, ((0, 16),))
    gate_cot = normal_values(part_splits[1], (TOKENS, FW), 1.0, 6.0, ((0, 16),))
    gate_weight = normal_values(arg_keys[2], (D, FW), (KMAX * TILE) ** -0.5, 0.15625, ((1, 16),))
    keep_mask = draw_keep_mask(jax.random.fold_in(arg_keys[4], 71), part)
    return {"tokens": tokens, "gate_cot": gate_cot, "gate_weight": gate_weight, "keep_mask": keep_mask}


def reference(tokens, gate_cot, gate_weight, keep_mask):
    tile_mask = jnp.repeat(jnp.repeat(keep_mask, TILE, axis=0), TILE, axis=1)
    pruned = jnp.where(tile_mask > 0, gate_weight, jnp.zeros_like(gate_weight))
    gate_out = jnp.dot(tokens, pruned, preferred_element_type=jnp.float32).astype(jnp.bfloat16)
    full = jnp.dot(tokens.T, gate_cot, preferred_element_type=jnp.float32)
    tiles = full.reshape(RT, TILE, CT, TILE).transpose(2, 0, 1, 3)
    kept_count = jnp.sum(keep_mask, axis=0)
    ordering = jnp.argsort(1 - keep_mask, axis=0, stable=True)[:KMAX].T.astype(jnp.int32)
    picked = jnp.take_along_axis(tiles, ordering[:, :, None, None], axis=1)
    valid = jnp.arange(KMAX)[None, :] < kept_count[:, None]
    picked = jnp.where(valid[:, :, None, None], picked, jnp.zeros_like(picked))
    return gate_out, picked.astype(jnp.bfloat16)
```

```python
import jax
import jax.numpy as jnp
from jax import lax
from jax.experimental import pallas as pl
from jax.experimental.pallas import tpu as pltpu
from jax.sharding import PartitionSpec as P

TILE = 128
RT = 32
KMAX = 12


def kept_lists(keep_mask):
    kept_count = jnp.sum(keep_mask, axis=0)
    ordering = jnp.argsort(1 - keep_mask, axis=0, stable=True)[:KMAX]
    kept_rows = ordering.T
    kept_valid = jnp.arange(KMAX)[None, :] < kept_count[:, None]
    return (kept_rows, kept_valid)


def column_tiles(gate_weight, kept_rows, kept_valid, column):
    strip = gate_weight[:, column * TILE : (column + 1) * TILE].reshape(RT, TILE, TILE)
    picked = jnp.take(strip, kept_rows[column], axis=0)
    picked = jnp.where(kept_valid[column][:, None, None], picked, jnp.zeros_like(picked))
    return picked.reshape(KMAX * TILE, TILE)


def general_path(tokens, gate_cot, gate_weight, keep_mask):
    local_width = gate_weight.shape[1]
    local_cols = local_width // TILE
    kept_rows, kept_valid = kept_lists(keep_mask)
    weight_cols = [
        column_tiles(gate_weight, kept_rows, kept_valid, column) for column in range(local_cols)
    ]
    cot_cols = lax.all_to_all(gate_cot, "fsdp", split_axis=1, concat_axis=0, tiled=True)
    total_rows = cot_cols.shape[0]

    def block_work(carry, piece, start):
        gate_all, grads = carry
        length = piece.shape[0]
        blocks = piece.reshape(length, RT, TILE)
        slope_piece = lax.dynamic_slice_in_dim(cot_cols, start, length, 0)
        outputs = []
        new_grads = []
        for column in range(local_cols):
            selected = jnp.take(blocks, kept_rows[column], axis=1).reshape(length, KMAX * TILE)
            outputs.append(
                jnp.dot(selected, weight_cols[column], preferred_element_type=jnp.float32)
            )
            slope_col = slope_piece[:, column * TILE : (column + 1) * TILE]
            grad_col = lax.dot_general(
                selected, slope_col, (((0,), (0,)), ((), ())), preferred_element_type=jnp.float32
            )
            new_grads.append(grad_col.reshape(KMAX, TILE, TILE))
        values = jnp.concatenate(outputs, axis=1).astype(jnp.bfloat16)
        gate_all = lax.dynamic_update_slice_in_dim(gate_all, values, start, 0)
        return (gate_all, grads + jnp.stack(new_grads, axis=0))

    initial = (
        jnp.zeros((total_rows, local_width), jnp.bfloat16),
        jnp.zeros((local_cols, KMAX, TILE, TILE), jnp.float32),
    )
    piece = lax.all_gather(tokens, "fsdp", axis=0, tiled=True)
    length = piece.shape[0]

    def one_block(index, inner):
        offset = index * 1024
        block_rows = lax.dynamic_slice_in_dim(piece, offset, 1024, 0)
        return block_work(inner, block_rows, offset)

    gate_cols, partial_tiles = lax.fori_loop(0, length // 1024, one_block, initial)
    gate_out = lax.all_to_all(gate_cols, "fsdp", split_axis=0, concat_axis=1, tiled=True)
    grad_tiles = jnp.where(
        kept_valid[:, :, None, None], partial_tiles, jnp.zeros_like(partial_tiles)
    )
    return (gate_out, grad_tiles.astype(jnp.bfloat16))


ZS = 4
PEERS = 16


def fused_kernel(
    rows_ref, valid_ref, tokens_ref, cot_ref, weight_ref, mask_ref,
    out_ref, grad_ref,
    tok, cot, w, gate, full,
    up_sem, down_sem, y_sem, sib_sem, ysib_sem, tok_recv,
    cot_send, cot_recv, gate_send, gate_recv, local_sem,
):
    me = lax.axis_index("fsdp")
    z = me // 4
    y = (me // 2) % 2
    c = me % 2
    width = weight_ref.shape[1]
    cols = width // TILE
    sibling = me + 1 - 2 * c
    partner = me + 2 - 4 * y

    def block(zz, yy, cc):
        return (zz * 2 + yy) * 2 + cc

    near = (z * (ZS - 1 - z)) // 2
    far_half = z // 2

    def order(k):
        f = k + near * (1 - 2 * k) * (1 - k // 2)
        return f + far_half * (ZS - 1 - 2 * f)

    def push(src, dst, send, recv, dev):
        return pltpu.make_async_remote_copy(
            src_ref=src, dst_ref=dst, send_sem=send, recv_sem=recv,
            device_id={"fsdp": dev}, device_id_type=pl.DeviceIdType.MESH,
        )

    barrier = pltpu.get_barrier_semaphore()

    def greet(o, carry):
        pl.semaphore_signal(
            barrier, inc=1, device_id={"fsdp": (me + o) % PEERS},
            device_id_type=pl.DeviceIdType.MESH,
        )
        return carry

    w_copy = pltpu.make_async_copy(weight_ref, w, local_sem.at[0])
    w_copy.start()
    tok_copy = pltpu.make_async_copy(tokens_ref, tok.at[me], local_sem.at[1])
    tok_copy.start()
    cot_copy = pltpu.make_async_copy(
        cot_ref.at[:, pl.ds(pl.multiple_of(me * width, width), width)], cot.at[me], local_sem.at[2]
    )
    cot_copy.start()
    lax.fori_loop(1, PEERS, greet, 0)
    pl.semaphore_wait(barrier, PEERS - 1)

    def tok_push(b, send, dev):
        return push(tok.at[b], tok.at[b], send, tok_recv.at[b], dev)

    def cot_push(o):
        d = (me + o) % PEERS
        return push(
            cot_ref.at[:, pl.ds(pl.multiple_of(d * width, width), width)],
            cot.at[me], cot_send.at[o], cot_recv.at[me], d,
        )

    def gate_push(b):
        return push(
            gate.at[b],
            out_ref.at[:, pl.ds(pl.multiple_of(me * width, width), width)],
            gate_send.at[b], gate_recv.at[me], b,
        )

    def own_copy():
        return pltpu.make_async_copy(
            gate.at[me],
            out_ref.at[:, pl.ds(pl.multiple_of(me * width, width), width)],
            local_sem.at[3],
        )

    def row_forward(k, act):
        zk = order(k)
        b = block(zk, y, c)

        @pl.when(jnp.logical_and(zk <= z, z < ZS - 1))
        def _():
            act(tok_push(b, up_sem.at[k], me + 4))

        @pl.when(jnp.logical_and(zk >= z, z > 0))
        def _():
            act(tok_push(b, down_sem.at[k], me - 4))

        act(tok_push(b, y_sem.at[k], partner))
        act(tok_push(b, sib_sem.at[k], sibling))

    def start(copy):
        copy.start()

    def wait_send(copy):
        copy.wait_send()

    def arrived(b):
        tok_push(b, up_sem.at[0], sibling).wait_recv()

    def gate_values(zk, yk):
        first = block(zk, yk, 0)
        arrived(block(zk, yk, 1 - c))

        def chunk(j, carry):
            at = pl.ds(pl.multiple_of(j * 256, 256), 256)
            lhs = tok[pl.ds(first, 2)].reshape(2 * tok.shape[1], tok.shape[2])
            val = jnp.dot(lhs, w[:, at], preferred_element_type=jnp.float32)
            gate[pl.ds(first, 2), :, at] = val.astype(jnp.bfloat16).reshape(2, tok.shape[1], 256)
            return carry

        lax.fori_loop(0, width // 256, chunk, 0)

        def out(cc, carry):
            b = first + cc

            @pl.when(b != me)
            def _():
                gate_push(b).start()

            return carry

        lax.fori_loop(0, 2, out, 0)

    tok_copy.wait()
    row_forward(0, start)

    def send_cot(o, carry):
        cot_push(o).start()
        return carry

    lax.fori_loop(1, PEERS, send_cot, 0)

    w_copy.wait()

    def prune(r, carry):
        at = pl.ds(pl.multiple_of(r * TILE, TILE), TILE)
        w[at, :] = w[at, :] * mask_ref[r]
        return carry

    lax.fori_loop(0, RT, prune, 0)

    def stage(k, carry):
        @pl.when(jnp.logical_and(k >= 1, k < ZS))
        def _():
            arrived(block(order(k), y, c))
            row_forward(k, start)

        @pl.when(k >= 1)
        def _():
            b = block(order(k - 1), 1 - y, c)
            arrived(b)
            tok_push(b, ysib_sem.at[k - 1], sibling).start()

        @pl.when(k < ZS)
        def _():
            gate_values(order(k), y)

        @pl.when(k == 0)
        def _():
            own_copy().start()

        @pl.when(k >= 1)
        def _():
            gate_values(order(k - 1), 1 - y)

        return carry

    lax.fori_loop(0, ZS + 1, stage, 0)

    cot_copy.wait()

    def wait_cot(o, carry):
        src = (me + o) % PEERS
        push(cot.at[src], cot.at[src], cot_send.at[o], cot_recv.at[src], src).wait_recv()
        return carry

    lax.fori_loop(1, PEERS, wait_cot, 0)

    def grad_chunk(i, carry):
        at = pl.ds(pl.multiple_of(i * 256, 256), 256)
        lhs = tok[:, :, at].reshape(PEERS * tok.shape[1], 256)
        rhs = cot[...].reshape(PEERS * tok.shape[1], width)
        val = lax.dot_general(
            lhs, rhs, (((0,), (0,)), ((), ())), preferred_element_type=jnp.float32
        )
        full[pl.ds(2 * i, 2)] = val.astype(jnp.bfloat16).reshape(2, TILE, width)
        return carry

    lax.fori_loop(0, RT // 2, grad_chunk, 0)

    def pick(k, carry):
        for col in range(cols):
            r = rows_ref[col * KMAX + k]
            keep = valid_ref[col * KMAX + k]
            tile = full[r, :, col * TILE : (col + 1) * TILE].astype(jnp.float32)
            tile = jnp.where(keep > 0, tile, jnp.zeros_like(tile))
            grad_ref[col, k] = tile.astype(jnp.bfloat16)
        return carry

    lax.fori_loop(0, KMAX, pick, 0)

    def finish(o, carry):
        peer = (me + o) % PEERS
        cot_push(o).wait_send()
        gate_push(peer).wait_send()
        push(
            gate.at[peer],
            out_ref.at[:, pl.ds(pl.multiple_of(peer * width, width), width)],
            gate_send.at[peer], gate_recv.at[peer], peer,
        ).wait_recv()
        return carry

    lax.fori_loop(1, PEERS, finish, 0)
    own_copy().wait()

    def finish_row(k, carry):
        row_forward(k, wait_send)
        tok_push(block(order(k), 1 - y, c), ysib_sem.at[k], sibling).wait_send()
        return carry

    lax.fori_loop(0, ZS, finish_row, 0)


def fused_path(tokens, gate_cot, gate_weight, keep_mask):
    length, depth = tokens.shape
    width = gate_weight.shape[1]
    cols = width // TILE
    kept_rows, kept_valid = kept_lists(keep_mask)
    mask = jnp.repeat(keep_mask, TILE, axis=1).astype(jnp.bfloat16)[:, None, :]
    bf = jnp.bfloat16
    dma = pltpu.SemaphoreType.DMA
    anywhere = pl.BlockSpec(memory_space=pl.ANY)
    return pl.pallas_call(
        fused_kernel,
        out_shape=(
            jax.ShapeDtypeStruct((length, PEERS * width), bf),
            jax.ShapeDtypeStruct((cols, KMAX, TILE, TILE), bf),
        ),
        in_specs=[
            pl.BlockSpec(memory_space=pltpu.SMEM),
            pl.BlockSpec(memory_space=pltpu.SMEM),
            anywhere, anywhere, anywhere,
            pl.BlockSpec(memory_space=pltpu.VMEM),
        ],
        out_specs=(anywhere, pl.BlockSpec(memory_space=pltpu.VMEM)),
        scratch_shapes=[
            pltpu.VMEM((PEERS, length, depth), bf),
            pltpu.VMEM((PEERS, length, width), bf),
            pltpu.VMEM((depth, width), bf),
            pltpu.VMEM((PEERS, length, width), bf),
            pltpu.VMEM((RT, TILE, width), bf),
            dma((ZS,)), dma((ZS,)), dma((ZS,)), dma((ZS,)), dma((ZS,)), dma((PEERS,)),
            dma((PEERS,)), dma((PEERS,)), dma((PEERS,)), dma((PEERS,)), dma((4,)),
        ],
        compiler_params=pltpu.CompilerParams(
            collective_id=0, has_side_effects=True, vmem_limit_bytes=60 * 1024 * 1024
        ),
    )(
        kept_rows.astype(jnp.int32).reshape(-1),
        kept_valid.astype(jnp.int32).reshape(-1),
        tokens, gate_cot, gate_weight, mask,
    )


def on_device(tokens, gate_cot, gate_weight, keep_mask):
    small = (tokens.shape, gate_weight.shape[1]) == ((128, RT * TILE), 8 * TILE)
    if lax.axis_size("fsdp") == PEERS and small:
        return fused_path(tokens, gate_cot, gate_weight, keep_mask)
    return general_path(tokens, gate_cot, gate_weight, keep_mask)


def solution(mesh):
    placed = (
        P(("group", "fsdp"), None),
        P(("group", "fsdp"), None),
        P(None, "fsdp"),
        P(None, "fsdp"),
    )
    return jax.shard_map(
        on_device,
        mesh=mesh,
        in_specs=placed,
        out_specs=(P(("group", "fsdp"), None), P(("group", "fsdp"), None, None, None)),
        check_vma=False,
    )
```

```python
import jax
import jax.numpy as jnp
from jax import lax
from jax.experimental import pallas as pl
from jax.experimental.pallas import tpu as pltpu
from jax.sharding import PartitionSpec as P

TILE = 128
RT = 32
KMAX = 12


def kept_lists(keep_mask):
    kept_count = jnp.sum(keep_mask, axis=0)
    ordering = jnp.argsort(1 - keep_mask, axis=0, stable=True)[:KMAX]
    kept_rows = ordering.T
    kept_valid = jnp.arange(KMAX)[None, :] < kept_count[:, None]
    return (kept_rows, kept_valid)


def column_tiles(gate_weight, kept_rows, kept_valid, column):
    strip = gate_weight[:, column * TILE : (column + 1) * TILE].reshape(RT, TILE, TILE)
    picked = jnp.take(strip, kept_rows[column], axis=0)
    picked = jnp.where(kept_valid[column][:, None, None], picked, jnp.zeros_like(picked))
    return picked.reshape(KMAX * TILE, TILE)


def general_path(tokens, gate_cot, gate_weight, keep_mask):
    local_width = gate_weight.shape[1]
    local_cols = local_width // TILE
    kept_rows, kept_valid = kept_lists(keep_mask)
    weight_cols = [
        column_tiles(gate_weight, kept_rows, kept_valid, column) for column in range(local_cols)
    ]
    cot_cols = lax.all_to_all(gate_cot, "fsdp", split_axis=1, concat_axis=0, tiled=True)
    total_rows = cot_cols.shape[0]

    def block_work(carry, piece, start):
        gate_all, grads = carry
        length = piece.shape[0]
        blocks = piece.reshape(length, RT, TILE)
        slope_piece = lax.dynamic_slice_in_dim(cot_cols, start, length, 0)
        outputs = []
        new_grads = []
        for column in range(local_cols):
            selected = jnp.take(blocks, kept_rows[column], axis=1).reshape(length, KMAX * TILE)
            outputs.append(
                jnp.dot(selected, weight_cols[column], preferred_element_type=jnp.float32)
            )
            slope_col = slope_piece[:, column * TILE : (column + 1) * TILE]
            grad_col = lax.dot_general(
                selected, slope_col, (((0,), (0,)), ((), ())), preferred_element_type=jnp.float32
            )
            new_grads.append(grad_col.reshape(KMAX, TILE, TILE))
        values = jnp.concatenate(outputs, axis=1).astype(jnp.bfloat16)
        gate_all = lax.dynamic_update_slice_in_dim(gate_all, values, start, 0)
        return (gate_all, grads + jnp.stack(new_grads, axis=0))

    initial = (
        jnp.zeros((total_rows, local_width), jnp.bfloat16),
        jnp.zeros((local_cols, KMAX, TILE, TILE), jnp.float32),
    )
    piece = lax.all_gather(tokens, "fsdp", axis=0, tiled=True)
    length = piece.shape[0]

    def one_block(index, inner):
        offset = index * 1024
        block_rows = lax.dynamic_slice_in_dim(piece, offset, 1024, 0)
        return block_work(inner, block_rows, offset)

    gate_cols, partial_tiles = lax.fori_loop(0, length // 1024, one_block, initial)
    gate_out = lax.all_to_all(gate_cols, "fsdp", split_axis=0, concat_axis=1, tiled=True)
    grad_tiles = jnp.where(
        kept_valid[:, :, None, None], partial_tiles, jnp.zeros_like(partial_tiles)
    )
    return (gate_out, grad_tiles.astype(jnp.bfloat16))


ZS = 4
PEERS = 16


def fused_kernel(
    rows_ref, valid_ref, tokens_ref, cot_ref, weight_ref, mask_ref,
    out_ref, grad_ref,
    tok, cot, w, gate, full,
    up_sem, down_sem, y_sem, sib_sem, ysib_sem, tok_recv,
    cot_send, cot_recv, gate_send, gate_recv, local_sem,
):
    me = lax.axis_index("fsdp")
    z = me // 4
    y = (me // 2) % 2
    c = me % 2
    width = weight_ref.shape[1]
    cols = width // TILE
    sibling = me + 1 - 2 * c
    partner = me + 2 - 4 * y

    def block(zz, yy, cc):
        return (zz * 2 + yy) * 2 + cc

    near = (z * (ZS - 1 - z)) // 2
    far_half = z // 2

    def order(k):
        f = k + near * (1 - 2 * k) * (1 - k // 2)
        return f + far_half * (ZS - 1 - 2 * f)

    def push(src, dst, send, recv, dev):
        return pltpu.make_async_remote_copy(
            src_ref=src, dst_ref=dst, send_sem=send, recv_sem=recv,
            device_id={"fsdp": dev}, device_id_type=pl.DeviceIdType.MESH,
        )

    barrier = pltpu.get_barrier_semaphore()

    def greet(o, carry):
        pl.semaphore_signal(
            barrier, inc=1, device_id={"fsdp": (me + o) % PEERS},
            device_id_type=pl.DeviceIdType.MESH,
        )
        return carry

    w_copy = pltpu.make_async_copy(weight_ref, w, local_sem.at[0])
    w_copy.start()
    tok_copy = pltpu.make_async_copy(tokens_ref, tok.at[me], local_sem.at[1])
    tok_copy.start()
    cot_copy = pltpu.make_async_copy(
        cot_ref.at[:, pl.ds(pl.multiple_of(me * width, width), width)], cot.at[me], local_sem.at[2]
    )
    cot_copy.start()
    lax.fori_loop(1, PEERS, greet, 0)
    pl.semaphore_wait(barrier, PEERS - 1)

    def tok_push(b, send, dev):
        return push(tok.at[b], tok.at[b], send, tok_recv.at[b], dev)

    def target(o):
        step = o - 1
        half = step // 8
        zh = (z // 2 + 1 + half) % 2
        j = (me % 8 + step % 8 + half) % 8
        return zh * 8 + j

    def cot_push(o):
        d = target(o)
        return push(
            cot_ref.at[:, pl.ds(pl.multiple_of(d * width, width), width)],
            cot.at[me], cot_send.at[o], cot_recv.at[me], d,
        )

    def gate_push(b):
        return push(
            gate.at[b],
            out_ref.at[:, pl.ds(pl.multiple_of(me * width, width), width)],
            gate_send.at[b], gate_recv.at[me], b,
        )

    def own_copy():
        return pltpu.make_async_copy(
            gate.at[me],
            out_ref.at[:, pl.ds(pl.multiple_of(me * width, width), width)],
            local_sem.at[3],
        )

    def row_forward(k, act):
        zk = order(k)
        b = block(zk, y, c)

        @pl.when(jnp.logical_and(zk <= z, z < ZS - 1))
        def _():
            act(tok_push(b, up_sem.at[k], me + 4))

        @pl.when(jnp.logical_and(zk >= z, z > 0))
        def _():
            act(tok_push(b, down_sem.at[k], me - 4))

        act(tok_push(b, y_sem.at[k], partner))
        act(tok_push(b, sib_sem.at[k], sibling))

    def start(copy):
        copy.start()

    def wait_send(copy):
        copy.wait_send()

    def arrived(b):
        tok_push(b, up_sem.at[0], sibling).wait_recv()

    def gate_values(zk, yk):
        first = block(zk, yk, 0)
        arrived(block(zk, yk, 1 - c))

        def chunk(j, carry):
            at = pl.ds(pl.multiple_of(j * 256, 256), 256)
            lhs = tok[pl.ds(first, 2)].reshape(2 * tok.shape[1], tok.shape[2])
            val = jnp.dot(lhs, w[:, at], preferred_element_type=jnp.float32)
            gate[pl.ds(first, 2), :, at] = val.astype(jnp.bfloat16).reshape(2, tok.shape[1], 256)
            return carry

        lax.fori_loop(0, width // 256, chunk, 0)

        def out(cc, carry):
            b = first + cc

            @pl.when(b != me)
            def _():
                gate_push(b).start()

            return carry

        lax.fori_loop(0, 2, out, 0)

    tok_copy.wait()
    row_forward(0, start)

    def send_cot(o, carry):
        cot_push(o).start()
        return carry


    w_copy.wait()

    def prune(r, carry):
        at = pl.ds(pl.multiple_of(r * TILE, TILE), TILE)
        w[at, :] = w[at, :] * mask_ref[r]
        return carry

    lax.fori_loop(0, RT, prune, 0)

    def stage(k, carry):
        @pl.when(jnp.logical_and(k >= 1, k < ZS))
        def _():
            arrived(block(order(k), y, c))
            row_forward(k, start)

        @pl.when(k >= 1)
        def _():
            b = block(order(k - 1), 1 - y, c)
            arrived(b)
            tok_push(b, ysib_sem.at[k - 1], sibling).start()

        for when, (lo, hi) in enumerate(zip((1, 4, 8, 12, 16)[:-1], (1, 4, 8, 12, 16)[1:])):

            @pl.when(k == when)
            def _(lo=lo, hi=hi):
                lax.fori_loop(lo, hi, send_cot, 0)

        @pl.when(k < ZS)
        def _():
            gate_values(order(k), y)

        @pl.when(k == 0)
        def _():
            own_copy().start()

        @pl.when(k >= 1)
        def _():
            gate_values(order(k - 1), 1 - y)

        return carry

    lax.fori_loop(0, ZS + 1, stage, 0)

    cot_copy.wait()

    def wait_cot(o, carry):
        src = (me + o) % PEERS
        push(cot.at[src], cot.at[src], cot_send.at[o], cot_recv.at[src], src).wait_recv()
        return carry

    lax.fori_loop(1, PEERS, wait_cot, 0)

    def grad_chunk(i, carry):
        at = pl.ds(pl.multiple_of(i * 256, 256), 256)
        lhs = tok[:, :, at].reshape(PEERS * tok.shape[1], 256)
        rhs = cot[...].reshape(PEERS * tok.shape[1], width)
        val = lax.dot_general(
            lhs, rhs, (((0,), (0,)), ((), ())), preferred_element_type=jnp.float32
        )
        full[pl.ds(2 * i, 2)] = val.astype(jnp.bfloat16).reshape(2, TILE, width)
        return carry

    lax.fori_loop(0, RT // 2, grad_chunk, 0)

    def pick(k, carry):
        for col in range(cols):
            r = rows_ref[col * KMAX + k]
            keep = valid_ref[col * KMAX + k]
            tile = full[r, :, col * TILE : (col + 1) * TILE].astype(jnp.float32)
            tile = jnp.where(keep > 0, tile, jnp.zeros_like(tile))
            grad_ref[col, k] = tile.astype(jnp.bfloat16)
        return carry

    lax.fori_loop(0, KMAX, pick, 0)

    def finish(o, carry):
        peer = (me + o) % PEERS
        cot_push(o).wait_send()
        gate_push(peer).wait_send()
        push(
            gate.at[peer],
            out_ref.at[:, pl.ds(pl.multiple_of(peer * width, width), width)],
            gate_send.at[peer], gate_recv.at[peer], peer,
        ).wait_recv()
        return carry

    lax.fori_loop(1, PEERS, finish, 0)
    own_copy().wait()

    def finish_row(k, carry):
        row_forward(k, wait_send)
        tok_push(block(order(k), 1 - y, c), ysib_sem.at[k], sibling).wait_send()
        return carry

    lax.fori_loop(0, ZS, finish_row, 0)


def fused_path(tokens, gate_cot, gate_weight, keep_mask):
    length, depth = tokens.shape
    width = gate_weight.shape[1]
    cols = width // TILE
    kept_rows, kept_valid = kept_lists(keep_mask)
    mask = jnp.repeat(keep_mask, TILE, axis=1).astype(jnp.bfloat16)[:, None, :]
    bf = jnp.bfloat16
    dma = pltpu.SemaphoreType.DMA
    anywhere = pl.BlockSpec(memory_space=pl.ANY)
    return pl.pallas_call(
        fused_kernel,
        out_shape=(
            jax.ShapeDtypeStruct((length, PEERS * width), bf),
            jax.ShapeDtypeStruct((cols, KMAX, TILE, TILE), bf),
        ),
        in_specs=[
            pl.BlockSpec(memory_space=pltpu.SMEM),
            pl.BlockSpec(memory_space=pltpu.SMEM),
            anywhere, anywhere, anywhere,
            pl.BlockSpec(memory_space=pltpu.VMEM),
        ],
        out_specs=(anywhere, pl.BlockSpec(memory_space=pltpu.VMEM)),
        scratch_shapes=[
            pltpu.VMEM((PEERS, length, depth), bf),
            pltpu.VMEM((PEERS, length, width), bf),
            pltpu.VMEM((depth, width), bf),
            pltpu.VMEM((PEERS, length, width), bf),
            pltpu.VMEM((RT, TILE, width), bf),
            dma((ZS,)), dma((ZS,)), dma((ZS,)), dma((ZS,)), dma((ZS,)), dma((PEERS,)),
            dma((PEERS,)), dma((PEERS,)), dma((PEERS,)), dma((PEERS,)), dma((4,)),
        ],
        compiler_params=pltpu.CompilerParams(
            collective_id=0, has_side_effects=True, vmem_limit_bytes=60 * 1024 * 1024
        ),
    )(
        kept_rows.astype(jnp.int32).reshape(-1),
        kept_valid.astype(jnp.int32).reshape(-1),
        tokens, gate_cot, gate_weight, mask,
    )


def on_device(tokens, gate_cot, gate_weight, keep_mask):
    small = (tokens.shape, gate_weight.shape[1]) == ((128, RT * TILE), 8 * TILE)
    if lax.axis_size("fsdp") == PEERS and small:
        return fused_path(tokens, gate_cot, gate_weight, keep_mask)
    return general_path(tokens, gate_cot, gate_weight, keep_mask)


def solution(mesh):
    placed = (
        P(("group", "fsdp"), None),
        P(("group", "fsdp"), None),
        P(None, "fsdp"),
        P(None, "fsdp"),
    )
    return jax.shard_map(
        on_device,
        mesh=mesh,
        in_specs=placed,
        out_specs=(P(("group", "fsdp"), None), P(("group", "fsdp"), None, None, None)),
        check_vma=False,
    )
```

```python
import jax
import jax.numpy as jnp
from jax import lax
from jax.experimental import pallas as pl
from jax.experimental.pallas import tpu as pltpu
from jax.sharding import PartitionSpec as P

TILE = 128
RT = 32
KMAX = 12


def kept_lists(keep_mask):
    kept_count = jnp.sum(keep_mask, axis=0)
    ordering = jnp.argsort(1 - keep_mask, axis=0, stable=True)[:KMAX]
    kept_rows = ordering.T
    kept_valid = jnp.arange(KMAX)[None, :] < kept_count[:, None]
    return (kept_rows, kept_valid)


def column_tiles(gate_weight, kept_rows, kept_valid, column):
    strip = gate_weight[:, column * TILE : (column + 1) * TILE].reshape(RT, TILE, TILE)
    picked = jnp.take(strip, kept_rows[column], axis=0)
    picked = jnp.where(kept_valid[column][:, None, None], picked, jnp.zeros_like(picked))
    return picked.reshape(KMAX * TILE, TILE)


def general_path(tokens, gate_cot, gate_weight, keep_mask):
    local_width = gate_weight.shape[1]
    local_cols = local_width // TILE
    kept_rows, kept_valid = kept_lists(keep_mask)
    weight_cols = [
        column_tiles(gate_weight, kept_rows, kept_valid, column) for column in range(local_cols)
    ]
    cot_cols = lax.all_to_all(gate_cot, "fsdp", split_axis=1, concat_axis=0, tiled=True)
    total_rows = cot_cols.shape[0]

    def block_work(carry, piece, start):
        gate_all, grads = carry
        length = piece.shape[0]
        blocks = piece.reshape(length, RT, TILE)
        slope_piece = lax.dynamic_slice_in_dim(cot_cols, start, length, 0)
        outputs = []
        new_grads = []
        for column in range(local_cols):
            selected = jnp.take(blocks, kept_rows[column], axis=1).reshape(length, KMAX * TILE)
            outputs.append(
                jnp.dot(selected, weight_cols[column], preferred_element_type=jnp.float32)
            )
            slope_col = slope_piece[:, column * TILE : (column + 1) * TILE]
            grad_col = lax.dot_general(
                selected, slope_col, (((0,), (0,)), ((), ())), preferred_element_type=jnp.float32
            )
            new_grads.append(grad_col.reshape(KMAX, TILE, TILE))
        values = jnp.concatenate(outputs, axis=1).astype(jnp.bfloat16)
        gate_all = lax.dynamic_update_slice_in_dim(gate_all, values, start, 0)
        return (gate_all, grads + jnp.stack(new_grads, axis=0))

    initial = (
        jnp.zeros((total_rows, local_width), jnp.bfloat16),
        jnp.zeros((local_cols, KMAX, TILE, TILE), jnp.float32),
    )
    piece = lax.all_gather(tokens, "fsdp", axis=0, tiled=True)
    length = piece.shape[0]

    def one_block(index, inner):
        offset = index * 1024
        block_rows = lax.dynamic_slice_in_dim(piece, offset, 1024, 0)
        return block_work(inner, block_rows, offset)

    gate_cols, partial_tiles = lax.fori_loop(0, length // 1024, one_block, initial)
    gate_out = lax.all_to_all(gate_cols, "fsdp", split_axis=0, concat_axis=1, tiled=True)
    grad_tiles = jnp.where(
        kept_valid[:, :, None, None], partial_tiles, jnp.zeros_like(partial_tiles)
    )
    return (gate_out, grad_tiles.astype(jnp.bfloat16))


ZS = 4
PEERS = 16


def fused_kernel(
    rows_ref, valid_ref, place_ref, held_ref, tokens_ref, cot_ref, weight_ref, mask_ref,
    out_ref, grad_ref,
    tok, cot, w, gate, full,
    up_sem, down_sem, y_sem, sib_sem, ysib_sem, tok_recv,
    cot_send, cot_recv, gate_send, gate_recv, local_sem, tiles, tile_send, tile_recv,
):
    me = lax.axis_index("fsdp")
    g = lax.axis_index("group")
    mate = (me + PEERS // 2) % PEERS
    z = me // 4
    y = (me // 2) % 2
    c = me % 2
    width = weight_ref.shape[2]
    cols = width // TILE
    sibling = me + 1 - 2 * c
    partner = me + 2 - 4 * y

    def block(zz, yy, cc):
        return (zz * 2 + yy) * 2 + cc

    near = (z * (ZS - 1 - z)) // 2
    far_half = z // 2

    def order(k):
        f = k + near * (1 - 2 * k) * (1 - k // 2)
        return f + far_half * (ZS - 1 - 2 * f)

    def push(src, dst, send, recv, dev):
        return pltpu.make_async_remote_copy(
            src_ref=src, dst_ref=dst, send_sem=send, recv_sem=recv,
            device_id={"fsdp": dev}, device_id_type=pl.DeviceIdType.MESH,
        )

    barrier = pltpu.get_barrier_semaphore()

    def greet(o, carry):
        pl.semaphore_signal(
            barrier, inc=1, device_id={"fsdp": (me + o) % PEERS},
            device_id_type=pl.DeviceIdType.MESH,
        )
        return carry

    w_copy = pltpu.make_async_copy(weight_ref, w, local_sem.at[0])
    w_copy.start()
    tok_copy = pltpu.make_async_copy(tokens_ref, tok.at[me], local_sem.at[1])
    tok_copy.start()
    cot_copy = pltpu.make_async_copy(
        cot_ref.at[:, pl.ds(pl.multiple_of(me * width, width), width)], cot.at[me], local_sem.at[2]
    )
    cot_copy.start()
    lax.fori_loop(1, PEERS, greet, 0)
    pl.semaphore_signal(
        barrier, inc=1, device_id={"group": 1 - g}, device_id_type=pl.DeviceIdType.MESH
    )
    pl.semaphore_wait(barrier, PEERS)

    def tok_push(b, send, dev):
        return push(tok.at[b], tok.at[b], send, tok_recv.at[b], dev)

    def target(o):
        step = o - 1
        half = step // 8
        zh = (z // 2 + 1 + half) % 2
        j = (me % 8 + step % 8 + half) % 8
        return zh * 8 + j

    def cot_push(o):
        d = target(o)
        return push(
            cot_ref.at[:, pl.ds(pl.multiple_of(d * width, width), width)],
            cot.at[me], cot_send.at[o], cot_recv.at[me], d,
        )

    def out_columns(src):
        return out_ref.at[:, pl.ds(pl.multiple_of(src * width, width), width)]

    def gate_push(b, n):
        slot = (b + 8 * n) % PEERS
        src = (me + 8 * n) % PEERS
        return push(gate.at[slot], out_columns(src), gate_send.at[slot], gate_recv.at[src], b)

    def own_copy(n):
        src = (me + 8 * n) % PEERS
        return pltpu.make_async_copy(gate.at[src], out_columns(src), local_sem.at[3 + n])

    def tile_half(ref, which):
        return ref.at[:, pl.ds(which * (KMAX // 2), KMAX // 2)]

    def tile_push():
        return push(
            tile_half(grad_ref, g), tile_half(tiles, g), tile_send.at[0], tile_recv.at[0], mate
        )

    def tile_pass():
        return pltpu.make_async_remote_copy(
            src_ref=tile_half(tiles, g), dst_ref=tile_half(tiles, g),
            send_sem=tile_send.at[1], recv_sem=tile_recv.at[1],
            device_id={"group": 1 - g}, device_id_type=pl.DeviceIdType.MESH,
        )

    def row_forward(k, act):
        zk = order(k)
        b = block(zk, y, c)

        @pl.when(jnp.logical_and(zk <= z, z < ZS - 1))
        def _():
            act(tok_push(b, up_sem.at[k], me + 4))

        @pl.when(jnp.logical_and(zk >= z, z > 0))
        def _():
            act(tok_push(b, down_sem.at[k], me - 4))

        act(tok_push(b, y_sem.at[k], partner))
        act(tok_push(b, sib_sem.at[k], sibling))

    def start(copy):
        copy.start()

    def wait_send(copy):
        copy.wait_send()

    def arrived(b):
        tok_push(b, up_sem.at[0], sibling).wait_recv()

    def gate_values(zk, yk, n):
        first = block(zk, yk, 0)

        def chunk(j, carry):
            at = pl.ds(pl.multiple_of(j * 256, 256), 256)
            lhs = tok[pl.ds(first, 2)].reshape(2 * tok.shape[1], tok.shape[2])
            rhs = w[:, :, at].reshape(RT * TILE, 256)
            val = jnp.dot(lhs, rhs, preferred_element_type=jnp.float32)
            gate[pl.ds(first, 2), :, at] = val.astype(jnp.bfloat16).reshape(2, tok.shape[1], 256)
            return carry

        def mate_chunk(j, carry):
            at = pl.ds(pl.multiple_of(j * 256, 256), 256)
            lhs = tok[pl.ds(first, 2)].reshape(2 * tok.shape[1], tok.shape[2])
            rhs = full[:, :, at].reshape(RT * TILE, 256)
            val = jnp.dot(lhs, rhs, preferred_element_type=jnp.float32)
            slots = pl.ds((first + 8) % PEERS, 2)
            gate[slots, :, at] = val.astype(jnp.bfloat16).reshape(2, tok.shape[1], 256)
            return carry

        def out(cc, carry):
            b = first + cc

            @pl.when(b != me)
            def _():
                gate_push(b, n).start()

            @pl.when(b == me)
            def _():
                own_copy(n).start()

            return carry

        lax.fori_loop(0, width // 256, chunk if n == 0 else mate_chunk, 0)
        lax.fori_loop(0, 2, out, 0)

    tok_copy.wait()
    row_forward(0, start)

    def send_cot(o, carry):
        cot_push(o).start()
        return carry


    w_copy.wait()

    def prune(r, carry):
        w[r] = w[r] * mask_ref[r]
        return carry


    def pack(k, carry):
        for col in range(cols):
            r = rows_ref[col * KMAX + k]
            grad_ref[col, k] = w[r, :, col * TILE : (col + 1) * TILE]
        return carry

    lax.fori_loop(0, KMAX, pack, 0)
    tile_push().start()
    lax.fori_loop(0, RT, prune, 0)

    def stage(k, carry):
        @pl.when(jnp.logical_and(k >= 1, k < ZS))
        def _():
            arrived(block(order(k), y, c))
            row_forward(k, start)

        @pl.when(k >= 1)
        def _():
            b = block(order(k - 1), 1 - y, c)
            arrived(b)
            tok_push(b, ysib_sem.at[k - 1], sibling).start()

        for when, (lo, hi) in enumerate(zip((1, 4, 8, 12, 16)[:-1], (1, 4, 8, 12, 16)[1:])):

            @pl.when(k == when)
            def _(lo=lo, hi=hi):
                lax.fori_loop(lo, hi, send_cot, 0)

        @pl.when(k < ZS)
        def _():
            arrived(block(order(k), y, 1 - c))

        @pl.when(k >= 1)
        def _():
            arrived(block(order(k - 1), 1 - y, 1 - c))

        @pl.when(jnp.logical_and(k < ZS, order(k % ZS) // 2 == z // 2))
        def _():
            gate_values(order(k % ZS), y, 0)

        @pl.when(k == 1)
        def _():
            tile_push().wait_recv()
            tile_pass().start()

        back = (k + ZS - 1) % ZS

        @pl.when(jnp.logical_and(k >= 1, order(back) // 2 == z // 2))
        def _():
            gate_values(order(back), 1 - y, 0)

        return carry

    lax.fori_loop(0, ZS + 1, stage, 0)
    tile_pass().wait_recv()

    def spread(r, carry):
        for col in range(cols):
            p = place_ref[r * cols + col]
            tile = tiles[col, p].astype(jnp.float32)
            tile = jnp.where(held_ref[r * cols + col] > 0, tile, jnp.zeros_like(tile))
            full[r, :, col * TILE : (col + 1) * TILE] = tile.astype(jnp.bfloat16)
        return carry

    lax.fori_loop(0, RT, spread, 0)

    def mate_values(i, carry):
        gate_values((z // 2) * 2 + i // 2, i % 2, 1)
        return carry

    lax.fori_loop(0, ZS, mate_values, 0)
    tile_push().wait_send()
    tile_pass().wait_send()

    cot_copy.wait()

    def wait_cot(o, carry):
        src = (me + o) % PEERS
        push(cot.at[src], cot.at[src], cot_send.at[o], cot_recv.at[src], src).wait_recv()
        return carry

    lax.fori_loop(1, PEERS, wait_cot, 0)

    def grad_chunk(i, carry):
        at = pl.ds(pl.multiple_of(i * 256, 256), 256)
        lhs = tok[:, :, at].reshape(PEERS * tok.shape[1], 256)
        rhs = cot[...].reshape(PEERS * tok.shape[1], width)
        val = lax.dot_general(
            lhs, rhs, (((0,), (0,)), ((), ())), preferred_element_type=jnp.float32
        )
        full[pl.ds(2 * i, 2)] = val.astype(jnp.bfloat16).reshape(2, TILE, width)
        return carry

    lax.fori_loop(0, RT // 2, grad_chunk, 0)

    def pick(k, carry):
        for col in range(cols):
            r = rows_ref[col * KMAX + k]
            keep = valid_ref[col * KMAX + k]
            tile = full[r, :, col * TILE : (col + 1) * TILE].astype(jnp.float32)
            tile = jnp.where(keep > 0, tile, jnp.zeros_like(tile))
            grad_ref[col, k] = tile.astype(jnp.bfloat16)
        return carry

    lax.fori_loop(0, KMAX, pick, 0)

    def finish(o, carry):
        peer = (me + o) % PEERS
        cot_push(o).wait_send()
        return carry

    lax.fori_loop(1, PEERS, finish, 0)

    def finish_gate(o, carry):
        peer = (z // 2) * 8 + (me + o) % 8
        for n in range(2):
            gate_push(peer, n).wait_send()
            src = (peer + 8 * n) % PEERS
            push(
                gate.at[src], out_columns(src), gate_send.at[src], gate_recv.at[src], peer
            ).wait_recv()
        return carry

    lax.fori_loop(1, 8, finish_gate, 0)
    own_copy(0).wait()
    own_copy(1).wait()

    def finish_row(k, carry):
        row_forward(k, wait_send)
        tok_push(block(order(k), 1 - y, c), ysib_sem.at[k], sibling).wait_send()
        return carry

    lax.fori_loop(0, ZS, finish_row, 0)


def fused_path(tokens, gate_cot, gate_weight, keep_mask):
    length, depth = tokens.shape
    width = gate_weight.shape[1]
    cols = width // TILE
    kept_rows, kept_valid = kept_lists(keep_mask)
    mate_mask = lax.ppermute(
        keep_mask, "fsdp", [(i, (i + PEERS // 2) % PEERS) for i in range(PEERS)]
    )
    place = jnp.clip(jnp.cumsum(mate_mask, axis=0) - 1, 0, KMAX - 1)
    mask = jnp.repeat(keep_mask, TILE, axis=1).astype(jnp.bfloat16)[:, None, :]
    bf = jnp.bfloat16
    dma = pltpu.SemaphoreType.DMA
    anywhere = pl.BlockSpec(memory_space=pl.ANY)
    return pl.pallas_call(
        fused_kernel,
        out_shape=(
            jax.ShapeDtypeStruct((length, PEERS * width), bf),
            jax.ShapeDtypeStruct((cols, KMAX, TILE, TILE), bf),
        ),
        in_specs=[
            *[pl.BlockSpec(memory_space=pltpu.SMEM)] * 4,
            anywhere, anywhere, anywhere,
            pl.BlockSpec(memory_space=pltpu.VMEM),
        ],
        out_specs=(anywhere, pl.BlockSpec(memory_space=pltpu.VMEM)),
        scratch_shapes=[
            pltpu.VMEM((PEERS, length, depth), bf),
            pltpu.VMEM((PEERS, length, width), bf),
            pltpu.VMEM((RT, TILE, width), bf),
            pltpu.VMEM((PEERS, length, width), bf),
            pltpu.VMEM((RT, TILE, width), bf),
            dma((ZS,)), dma((ZS,)), dma((ZS,)), dma((ZS,)), dma((ZS,)), dma((PEERS,)),
            dma((PEERS,)), dma((PEERS,)), dma((PEERS,)), dma((PEERS,)), dma((5,)),
            pltpu.VMEM((cols, KMAX, TILE, TILE), bf), dma((2,)), dma((2,)),
        ],
        compiler_params=pltpu.CompilerParams(
            collective_id=0, has_side_effects=True, vmem_limit_bytes=60 * 1024 * 1024
        ),
    )(
        kept_rows.astype(jnp.int32).reshape(-1),
        kept_valid.astype(jnp.int32).reshape(-1),
        place.astype(jnp.int32).reshape(-1),
        mate_mask.reshape(-1),
        tokens, gate_cot, gate_weight.reshape(RT, TILE, width), mask,
    )


def on_device(tokens, gate_cot, gate_weight, keep_mask):
    small = (tokens.shape, gate_weight.shape[1]) == ((128, RT * TILE), 8 * TILE)
    if lax.axis_size("fsdp") == PEERS and small:
        return fused_path(tokens, gate_cot, gate_weight, keep_mask)
    return general_path(tokens, gate_cot, gate_weight, keep_mask)


def solution(mesh):
    placed = (
        P(("group", "fsdp"), None),
        P(("group", "fsdp"), None),
        P(None, "fsdp"),
        P(None, "fsdp"),
    )
    return jax.shard_map(
        on_device,
        mesh=mesh,
        in_specs=placed,
        out_specs=(P(("group", "fsdp"), None), P(("group", "fsdp"), None, None, None)),
        check_vma=False,
    )
```

```python
import jax
import jax.numpy as jnp
from jax import lax
from jax.experimental import pallas as pl
from jax.experimental.pallas import tpu as pltpu
from jax.sharding import PartitionSpec as P

TILE = 128
RT = 32
KMAX = 12


def kept_lists(keep_mask):
    kept_count = jnp.sum(keep_mask, axis=0)
    ordering = jnp.argsort(1 - keep_mask, axis=0, stable=True)[:KMAX]
    kept_rows = ordering.T
    kept_valid = jnp.arange(KMAX)[None, :] < kept_count[:, None]
    return (kept_rows, kept_valid)


def column_tiles(gate_weight, kept_rows, kept_valid, column):
    strip = gate_weight[:, column * TILE : (column + 1) * TILE].reshape(RT, TILE, TILE)
    picked = jnp.take(strip, kept_rows[column], axis=0)
    picked = jnp.where(kept_valid[column][:, None, None], picked, jnp.zeros_like(picked))
    return picked.reshape(KMAX * TILE, TILE)


def general_path(tokens, gate_cot, gate_weight, keep_mask):
    local_width = gate_weight.shape[1]
    local_cols = local_width // TILE
    kept_rows, kept_valid = kept_lists(keep_mask)
    weight_cols = [
        column_tiles(gate_weight, kept_rows, kept_valid, column) for column in range(local_cols)
    ]
    cot_cols = lax.all_to_all(gate_cot, "fsdp", split_axis=1, concat_axis=0, tiled=True)
    total_rows = cot_cols.shape[0]

    def block_work(carry, piece, start):
        gate_all, grads = carry
        length = piece.shape[0]
        blocks = piece.reshape(length, RT, TILE)
        slope_piece = lax.dynamic_slice_in_dim(cot_cols, start, length, 0)
        outputs = []
        new_grads = []
        for column in range(local_cols):
            selected = jnp.take(blocks, kept_rows[column], axis=1).reshape(length, KMAX * TILE)
            outputs.append(
                jnp.dot(selected, weight_cols[column], preferred_element_type=jnp.float32)
            )
            slope_col = slope_piece[:, column * TILE : (column + 1) * TILE]
            grad_col = lax.dot_general(
                selected, slope_col, (((0,), (0,)), ((), ())), preferred_element_type=jnp.float32
            )
            new_grads.append(grad_col.reshape(KMAX, TILE, TILE))
        values = jnp.concatenate(outputs, axis=1).astype(jnp.bfloat16)
        gate_all = lax.dynamic_update_slice_in_dim(gate_all, values, start, 0)
        return (gate_all, grads + jnp.stack(new_grads, axis=0))

    initial = (
        jnp.zeros((total_rows, local_width), jnp.bfloat16),
        jnp.zeros((local_cols, KMAX, TILE, TILE), jnp.float32),
    )
    piece = lax.all_gather(tokens, "fsdp", axis=0, tiled=True)
    length = piece.shape[0]

    def one_block(index, inner):
        offset = index * 1024
        block_rows = lax.dynamic_slice_in_dim(piece, offset, 1024, 0)
        return block_work(inner, block_rows, offset)

    gate_cols, partial_tiles = lax.fori_loop(0, length // 1024, one_block, initial)
    gate_out = lax.all_to_all(gate_cols, "fsdp", split_axis=0, concat_axis=1, tiled=True)
    grad_tiles = jnp.where(
        kept_valid[:, :, None, None], partial_tiles, jnp.zeros_like(partial_tiles)
    )
    return (gate_out, grad_tiles.astype(jnp.bfloat16))


ZS = 4
PEERS = 16


def fused_kernel(
    rows_ref, valid_ref, tokens_ref, cot_ref, weight_ref, mask_ref,
    out_ref, grad_ref,
    tok, cot, w, gate, full,
    up_sem, down_sem, y_sem, sib_sem, ysib_sem, tok_recv,
    cot_send, cot_recv, gate_send, gate_recv, local_sem,
):
    me = lax.axis_index("fsdp")
    z = me // 4
    y = (me // 2) % 2
    c = me % 2
    width = weight_ref.shape[1]
    cols = width // TILE
    sibling = me + 1 - 2 * c
    partner = me + 2 - 4 * y

    def block(zz, yy, cc):
        return (zz * 2 + yy) * 2 + cc

    near = (z * (ZS - 1 - z)) // 2
    far_half = z // 2

    def order(k):
        f = k + near * (1 - 2 * k) * (1 - k // 2)
        return f + far_half * (ZS - 1 - 2 * f)

    def push(src, dst, send, recv, dev):
        return pltpu.make_async_remote_copy(
            src_ref=src, dst_ref=dst, send_sem=send, recv_sem=recv,
            device_id={"fsdp": dev}, device_id_type=pl.DeviceIdType.MESH,
        )

    barrier = pltpu.get_barrier_semaphore()

    def greet(o, carry):
        pl.semaphore_signal(
            barrier, inc=1, device_id={"fsdp": (me + o) % PEERS},
            device_id_type=pl.DeviceIdType.MESH,
        )
        return carry

    w_copy = pltpu.make_async_copy(weight_ref, w, local_sem.at[0])
    w_copy.start()
    tok_copy = pltpu.make_async_copy(tokens_ref, tok.at[me], local_sem.at[1])
    tok_copy.start()
    cot_copy = pltpu.make_async_copy(
        cot_ref.at[:, pl.ds(pl.multiple_of(me * width, width), width)], cot.at[me], local_sem.at[2]
    )
    cot_copy.start()
    lax.fori_loop(1, PEERS, greet, 0)
    pl.semaphore_wait(barrier, PEERS - 1)

    def tok_push(b, send, dev):
        return push(tok.at[b], tok.at[b], send, tok_recv.at[b], dev)

    def target(o):
        step = o - 1
        half = step // 8
        zh = (z // 2 + 1 + half) % 2
        j = (me % 8 + step % 8 + half) % 8
        return zh * 8 + j

    def cot_push(o):
        d = target(o)
        return push(
            cot_ref.at[:, pl.ds(pl.multiple_of(d * width, width), width)],
            cot.at[me], cot_send.at[o], cot_recv.at[me], d,
        )

    def gate_push(b):
        return push(
            gate.at[b],
            out_ref.at[:, pl.ds(pl.multiple_of(me * width, width), width)],
            gate_send.at[b], gate_recv.at[me], b,
        )

    def own_copy():
        return pltpu.make_async_copy(
            gate.at[me],
            out_ref.at[:, pl.ds(pl.multiple_of(me * width, width), width)],
            local_sem.at[3],
        )

    def row_forward(k, act):
        zk = order(k)
        b = block(zk, y, c)

        @pl.when(jnp.logical_and(zk <= z, z < ZS - 1))
        def _():
            act(tok_push(b, up_sem.at[k], me + 4))

        @pl.when(jnp.logical_and(zk >= z, z > 0))
        def _():
            act(tok_push(b, down_sem.at[k], me - 4))

        act(tok_push(b, y_sem.at[k], partner))
        act(tok_push(b, sib_sem.at[k], sibling))

    def start(copy):
        copy.start()

    def wait_send(copy):
        copy.wait_send()

    def arrived(b):
        tok_push(b, up_sem.at[0], sibling).wait_recv()

    def gate_values(zk, yk):
        first = block(zk, yk, 0)
        arrived(block(zk, yk, 1 - c))

        def chunk(j, carry):
            at = pl.ds(pl.multiple_of(j * 256, 256), 256)
            lhs = tok[pl.ds(first, 2)].reshape(2 * tok.shape[1], tok.shape[2])
            val = jnp.dot(lhs, w[:, at], preferred_element_type=jnp.float32)
            gate[pl.ds(first, 2), :, at] = val.astype(jnp.bfloat16).reshape(2, tok.shape[1], 256)
            return carry

        lax.fori_loop(0, width // 256, chunk, 0)

        def out(cc, carry):
            b = first + cc

            @pl.when(b != me)
            def _():
                gate_push(b).start()

            return carry

        lax.fori_loop(0, 2, out, 0)

    tok_copy.wait()
    row_forward(0, start)

    def send_cot(o, carry):
        cot_push(o).start()
        return carry


    w_copy.wait()

    def prune(r, carry):
        at = pl.ds(pl.multiple_of(r * TILE, TILE), TILE)
        w[at, :] = w[at, :] * mask_ref[r]
        return carry

    lax.fori_loop(0, RT, prune, 0)

    def stage(k, carry):
        @pl.when(jnp.logical_and(k >= 1, k < ZS))
        def _():
            arrived(block(order(k), y, c))
            row_forward(k, start)

        @pl.when(k >= 1)
        def _():
            b = block(order(k - 1), 1 - y, c)
            arrived(b)
            tok_push(b, ysib_sem.at[k - 1], sibling).start()

        for when, (lo, hi) in enumerate(zip((1, 4, 8, 12, 16)[:-1], (1, 4, 8, 12, 16)[1:])):

            @pl.when(k == when)
            def _(lo=lo, hi=hi):
                lax.fori_loop(lo, hi, send_cot, 0)

        @pl.when(k < ZS)
        def _():
            gate_values(order(k), y)

        @pl.when(k == 0)
        def _():
            own_copy().start()

        @pl.when(k >= 1)
        def _():
            gate_values(order(k - 1), 1 - y)

        return carry

    lax.fori_loop(0, ZS + 1, stage, 0)

    cot_copy.wait()

    def wait_cot(o, carry):
        src = (me + o) % PEERS
        push(cot.at[src], cot.at[src], cot_send.at[o], cot_recv.at[src], src).wait_recv()
        return carry

    lax.fori_loop(1, PEERS, wait_cot, 0)

    def grad_chunk(i, carry):
        at = pl.ds(pl.multiple_of(i * 256, 256), 256)
        lhs = tok[:, :, at].reshape(PEERS * tok.shape[1], 256)
        rhs = cot[...].reshape(PEERS * tok.shape[1], width)
        val = lax.dot_general(
            lhs, rhs, (((0,), (0,)), ((), ())), preferred_element_type=jnp.float32
        )
        full[pl.ds(2 * i, 2)] = val.astype(jnp.bfloat16).reshape(2, TILE, width)
        return carry

    lax.fori_loop(0, RT // 2, grad_chunk, 0)

    def pick(k, carry):
        for col in range(cols):
            r = rows_ref[col * KMAX + k]
            keep = valid_ref[col * KMAX + k]
            tile = full[r, :, col * TILE : (col + 1) * TILE].astype(jnp.float32)
            tile = jnp.where(keep > 0, tile, jnp.zeros_like(tile))
            grad_ref[col, k] = tile.astype(jnp.bfloat16)
        return carry

    lax.fori_loop(0, KMAX, pick, 0)

    def finish(o, carry):
        peer = (me + o) % PEERS
        cot_push(o).wait_send()
        gate_push(peer).wait_send()
        push(
            gate.at[peer],
            out_ref.at[:, pl.ds(pl.multiple_of(peer * width, width), width)],
            gate_send.at[peer], gate_recv.at[peer], peer,
        ).wait_recv()
        return carry

    lax.fori_loop(1, PEERS, finish, 0)
    own_copy().wait()

    def finish_row(k, carry):
        row_forward(k, wait_send)
        tok_push(block(order(k), 1 - y, c), ysib_sem.at[k], sibling).wait_send()
        return carry

    lax.fori_loop(0, ZS, finish_row, 0)


def fused_path(tokens, gate_cot, gate_weight, keep_mask):
    length, depth = tokens.shape
    width = gate_weight.shape[1]
    cols = width // TILE
    running = jnp.cumsum(keep_mask, axis=0)
    places = jnp.arange(KMAX)
    ahead = running.T[:, None, :] <= places[None, :, None]
    kept_rows = jnp.minimum(jnp.sum(ahead.astype(jnp.int32), axis=2), RT - 1)
    kept_valid = places[None, :] < running[-1][:, None]
    mask = jnp.repeat(keep_mask, TILE, axis=1).astype(jnp.bfloat16)[:, None, :]
    bf = jnp.bfloat16
    dma = pltpu.SemaphoreType.DMA
    anywhere = pl.BlockSpec(memory_space=pl.ANY)
    return pl.pallas_call(
        fused_kernel,
        out_shape=(
            jax.ShapeDtypeStruct((length, PEERS * width), bf),
            jax.ShapeDtypeStruct((cols, KMAX, TILE, TILE), bf),
        ),
        in_specs=[
            pl.BlockSpec(memory_space=pltpu.SMEM),
            pl.BlockSpec(memory_space=pltpu.SMEM),
            anywhere, anywhere, anywhere,
            pl.BlockSpec(memory_space=pltpu.VMEM),
        ],
        out_specs=(anywhere, pl.BlockSpec(memory_space=pltpu.VMEM)),
        scratch_shapes=[
            pltpu.VMEM((PEERS, length, depth), bf),
            pltpu.VMEM((PEERS, length, width), bf),
            pltpu.VMEM((depth, width), bf),
            pltpu.VMEM((PEERS, length, width), bf),
            pltpu.VMEM((RT, TILE, width), bf),
            dma((ZS,)), dma((ZS,)), dma((ZS,)), dma((ZS,)), dma((ZS,)), dma((PEERS,)),
            dma((PEERS,)), dma((PEERS,)), dma((PEERS,)), dma((PEERS,)), dma((4,)),
        ],
        compiler_params=pltpu.CompilerParams(
            collective_id=0, has_side_effects=True, vmem_limit_bytes=60 * 1024 * 1024
        ),
    )(
        kept_rows.astype(jnp.int32).reshape(-1),
        kept_valid.astype(jnp.int32).reshape(-1),
        tokens, gate_cot, gate_weight, mask,
    )


def on_device(tokens, gate_cot, gate_weight, keep_mask):
    small = (tokens.shape, gate_weight.shape[1]) == ((128, RT * TILE), 8 * TILE)
    if lax.axis_size("fsdp") == PEERS and small:
        return fused_path(tokens, gate_cot, gate_weight, keep_mask)
    return general_path(tokens, gate_cot, gate_weight, keep_mask)


def solution(mesh):
    placed = (
        P(("group", "fsdp"), None),
        P(("group", "fsdp"), None),
        P(None, "fsdp"),
        P(None, "fsdp"),
    )
    return jax.shard_map(
        on_device,
        mesh=mesh,
        in_specs=placed,
        out_specs=(P(("group", "fsdp"), None), P(("group", "fsdp"), None, None, None)),
        check_vma=False,
    )
```
